512 devices in a mesh: section: 8 (over x, core), dp: 64 (over y, z).
Axes of the slice: x: 4, y: 4, z: 16, core: 2. Of those that a mesh axis runs over, the one named last changes fastest.
Arguments:
- stream_in: bfloat16 [128, 8192], P(None, 'dp'), may hold values from -6 to 6
- gains: float32 [8, 8192], P('section'), may hold values from 0.5 to 1.5
- weights: bfloat16 [8, 8192, 8192], P('section', 'dp'), may hold values from -6 to 6
- masks: int32 [8, 8192, 128], P('section', 'dp'), may hold values 0 or 1
- inv_hessian: float32 [8, 64, 128, 128], P('section', 'dp'), may hold values from -0.025 to 3.2
Outputs:
- stream_out: bfloat16 [8, 128, 8192], P('section', None, 'dp')
- refitted: bfloat16 [8, 8192, 8192], P('section', 'dp')
The draws below stay inside these ranges and needn't reach their ends.
All inputs are finite; a program needn't handle non-finite values. No bound on the sum of `masks` on one device may be relied on, other than what follows from the above.
Results may differ from the reference program's by a relative error of at most 0.015.
Values may be sent and summed in bfloat16 or wider, within the bound.
No kernel may reach another device: no remote copies, remote signals or barrier semaphores. Data moves between devices by JAX's collectives and lax.ppermute only.
A program may use at most 64 MiB of HBM per device.

```python
import jax
import jax.numpy as jnp
from jax import lax

D = 8192
BLOCK = 128
TOKENS = 128
SECTIONS = 8
NB = 64
N_SECTION = 8


def draw_inv_hessian(key, part):
    first, second = jax.random.split(jax.random.fold_in(key, 17))
    diagonal = jax.random.uniform(first, (SECTIONS, NB, BLOCK), jnp.float32, 1.6, 3.2)
    spread = jax.random.uniform(second, (SECTIONS, NB, BLOCK, BLOCK), jnp.float32, -0.025, 0.025)
    symmetric = 0.5 * (spread + jnp.swapaxes(spread, 2, 3))
    identity = jnp.eye(BLOCK, dtype=jnp.float32)
    return symmetric * (1.0 - identity) + diagonal[..., None] * identity


def with_ends(drawn, key, low, top_value):
    place = [jax.random.randint(jax.random.fold_in(key, axis), (), 0, length) for axis, length in enumerate(drawn.shape)]
    longest = drawn.shape.index(max(drawn.shape))
    neighbour = place[:longest] + [(place[longest] + 1) % drawn.shape[longest]] + place[longest + 1:]
    return drawn.at[tuple(place)].set(low).at[tuple(neighbour)].set(top_value)


def steps_of(own_key, extent, pieces, low, largest):
    def one(position, blocks):
        heights = jax.random.uniform(jax.random.fold_in(jax.random.fold_in(own_key, 6), position), (blocks,), jnp.float32, low / len(pieces), largest / len(pieces))
        return jnp.repeat(jnp.exp(heights), extent[position] // blocks).reshape((-1,) + (1,) * (len(extent) - position - 1))

    level = one(*pieces[0])
    for cut in pieces[1:]:
        level = level * one(*cut)
    return level


def gaussian(key, shape, scale, limit, shards=(), kind=jnp.bfloat16):
    values = scale * jax.random.normal(key, shape, jnp.float32)
    if shards:
        values = values * steps_of(key, shape, shards, -0.22, 0.18)
    return jnp.clip(values, -limit, limit).astype(kind)


def setup_inputs(seed: int = 0) -> dict:
    seeds = jax.random.split(jax.random.key(seed), 6)
    stream_in = gaussian(seeds[0], (TOKENS, D), 1.0, 6.0, ((1, 64),))
    gains = jnp.clip(1.0 + 0.1 * jax.random.normal(seeds[1], (SECTIONS, D), jnp.float32), 0.5, 1.5)
    weights = gaussian(seeds[2], (SECTIONS, D, D), 1.0, 6.0, ((0, 8), (1, 64)))
    masks = with_ends((jax.random.randint(seeds[3], (SECTIONS, D, 2 * NB), 0, 2) < 1).astype(jnp.int32), jax.random.fold_in(seeds[3], 1), 0, 1)
    inv_hessian = draw_inv_hessian(jax.random.fold_in(seeds[5], 71), 0)
    return dict(stream_in=stream_in, gains=gains, weights=weights, masks=masks, inv_hessian=inv_hessian)


def reference(stream_in, gains, weights, masks, inv_hessian):
    stream = stream_in
    outputs = []
    refits = []
    for layer in range(N_SECTION):
        widened = stream.astype(jnp.float32)
        mean_square = lax.optimization_barrier(jnp.mean(widened * widened, axis=1, keepdims=True))
        normed = (widened * lax.rsqrt(mean_square + 1e-05) * gains[layer]).astype(jnp.bfloat16)
        keep = jnp.repeat(masks[layer], BLOCK // 2, axis=1)
        kept_rows = weights[layer] * keep.astype(jnp.bfloat16)
        projected = jnp.dot(normed, kept_rows.T, preferred_element_type=jnp.float32) * D ** (-0.5)
        stream = (widened + projected).astype(jnp.bfloat16)
        outputs.append(stream)
        blocks = normed.astype(jnp.float32).reshape(TOKENS, NB, BLOCK)
        gram_block = jnp.einsum('tbi,tbj->bij', blocks, blocks, precision=lax.Precision.HIGHEST)
        hessian = gram_block * (1.0 / TOKENS)
        removed = weights[layer].astype(jnp.float32) * (1 - keep).astype(jnp.float32)
        removed = removed.reshape(D, NB, BLOCK)
        gradient = jnp.einsum('rbi,bij->rbj', removed, hessian, precision=lax.Precision.HIGHEST)
        update_step = jnp.einsum('rbi,bij->rbj', gradient, inv_hessian[layer], precision=lax.Precision.HIGHEST)
        refitted = keep.astype(jnp.float32) * (weights[layer].astype(jnp.float32) + update_step.reshape(D, D))
        refits.append(refitted.astype(jnp.bfloat16))
    return (jnp.stack(outputs), jnp.stack(refits))
```

```python
import functools

import jax
import jax.numpy as jnp
from jax import lax
from jax.experimental import pallas as pl
from jax.experimental.pallas import tpu as pltpu
from jax.sharding import PartitionSpec as P

D = 8192
BLOCK = 128
HALF = BLOCK // 2
ROWS = 128
TOKENS = 128
Y = 4
Z = 16
SECTIONS = 8
SPAN = Z * BLOCK
SCALE = D ** (-0.5)
EPS = 1e-05
AXES = ("section", "dp")
Y_GROUPS = [[y * Z + z for y in range(Y)] for z in range(Z)]
Z_GROUPS = [[y * Z + z for z in range(Z)] for y in range(Y)]
BF = jnp.bfloat16
F32 = jnp.float32
NT = (((1,), (1,)), ((), ()))
TN = (((0,), (0,)), ((), ()))


def spread(masks, first, width):
    column = lax.broadcasted_iota(jnp.int32, (masks.shape[1], width), 1) + first
    row = lax.broadcasted_iota(jnp.int32, (masks.shape[1], width), 0)
    low = row * HALF
    chosen = ((column >= low) & (column < low + HALF)).astype(F32).astype(BF)
    return jnp.dot(masks.astype(F32).astype(BF), chosen, preferred_element_type=F32)


def keep_kernel(weights_ref, masks_ref, kept_ref):
    width = weights_ref.shape[1]
    keep = spread(masks_ref[...], pl.program_id(0) * width, width)
    kept_ref[0] = (weights_ref[...].astype(F32) * keep).astype(BF)


def keep_weights(weights, masks):
    return pl.pallas_call(
        keep_kernel,
        grid=(Y,),
        in_specs=[
            pl.BlockSpec((ROWS, SPAN), lambda i: (0, i)),
            pl.BlockSpec((ROWS, masks.shape[1]), lambda i: (0, 0)),
        ],
        out_specs=pl.BlockSpec((1, ROWS, SPAN), lambda i: (i, 0, 0)),
        out_shape=jax.ShapeDtypeStruct((Y, ROWS, SPAN), BF),
        name="keep_weights",
    )(weights, masks)


def layer_kernel(x_ref, own_ref, gain_ref, kept_ref, *refs):
    outs, scaled = refs[:Y], refs[Y]
    squares = jnp.zeros((TOKENS, BLOCK), F32)
    for j in range(Z):
        x = x_ref[j].astype(F32)
        squares = squares + x * x
        scaled[:, j * BLOCK : (j + 1) * BLOCK] = (
            x * gain_ref[:, j * BLOCK : (j + 1) * BLOCK]
        ).astype(BF)
    total = jnp.sum(squares, axis=1, keepdims=True)
    high = total.astype(BF)
    low = (total - high.astype(F32)).astype(BF)
    lane = lax.broadcasted_iota(jnp.int32, (TOKENS, BLOCK), 1)
    both = jnp.where(
        lane < HALF,
        jnp.broadcast_to(high.astype(F32), (TOKENS, BLOCK)),
        jnp.broadcast_to(low.astype(F32), (TOKENS, BLOCK)),
    ).astype(BF)
    partial = lax.dot_general(scaled[...], kept_ref[...], NT, preferred_element_type=F32)
    for k in range(Y):
        outs[k][:, :BLOCK] = (partial[:, k * BLOCK : (k + 1) * BLOCK] * SCALE).astype(BF)
        outs[k][:, BLOCK : 2 * BLOCK] = both
    outs[0][:, 2 * BLOCK :] = own_ref[...]


def layer(x, own, gain, kept):
    widths = [3 * BLOCK] + [2 * BLOCK] * (Y - 1)
    return pl.pallas_call(
        layer_kernel,
        out_shape=[jax.ShapeDtypeStruct((TOKENS, w), BF) for w in widths],
        scratch_shapes=[pltpu.VMEM((TOKENS, SPAN), BF)],
        name="layer",
    )(x, own, gain, kept)


def join(parts):
    projected = sum(p[:, :BLOCK].astype(F32) for p in parts)
    total = sum(
        p[:, BLOCK : BLOCK + 1].astype(F32) + p[:, BLOCK + HALF : BLOCK + HALF + 1].astype(F32)
        for p in parts
    )
    inverse = lax.rsqrt(total * (1.0 / D) + EPS)
    return (parts[0][:, 2 * BLOCK :].astype(F32) + projected * inverse).astype(BF)


PER_STEP = 8
WIDTH = PER_STEP * BLOCK


def refit_kernel(x_ref, own_ref, gain_ref, weights_ref, masks_ref, inverse_ref, stream_ref, refit_ref, norm, acc):
    step = pl.program_id(0)

    @pl.when(step == 0)
    def _():
        def add(b, squares):
            x = x_ref[b].astype(F32)
            return squares + x * x

        squares = lax.fori_loop(0, D // BLOCK, add, jnp.zeros((TOKENS, BLOCK), F32), unroll=8)
        total = jnp.sum(squares, axis=1, keepdims=True)
        norm[...] = jnp.broadcast_to(lax.rsqrt(total * (1.0 / D) + EPS), (TOKENS, BLOCK))
        acc[...] = jnp.zeros((TOKENS, ROWS), F32)

    keep = spread(masks_ref[...], step * WIDTH, WIDTH)
    scale = norm[...]
    projected = acc[...]
    for j in range(PER_STEP):
        cut = slice(j * BLOCK, (j + 1) * BLOCK)
        x = x_ref[step * PER_STEP + j].astype(F32)
        normed = (x * scale * gain_ref[:, cut]).astype(BF)
        gram = lax.dot_general(normed, normed, TN, preferred_element_type=F32)
        hessian = (gram * (1.0 / TOKENS)).astype(BF)
        product = jnp.dot(hessian, inverse_ref[j], preferred_element_type=F32).astype(BF)
        weights = weights_ref[:, cut].astype(F32)
        kept = weights * keep[:, cut]
        removed = (weights - kept).astype(BF)
        update = jnp.dot(removed, product, preferred_element_type=F32)
        refit_ref[:, cut] = (keep[:, cut] * (weights + update)).astype(BF)
        projected = projected + lax.dot_general(
            normed, kept.astype(BF), NT, preferred_element_type=F32
        )
    acc[...] = projected

    @pl.when(step == D // WIDTH - 1)
    def _():
        stream_ref[...] = (own_ref[...].astype(F32) + projected * SCALE).astype(BF)


def refit(x, own, gain, weights, masks, inverse):
    whole = lambda *shape: pl.BlockSpec(shape, lambda i: (0,) * len(shape))
    return pl.pallas_call(
        refit_kernel,
        grid=(D // WIDTH,),
        in_specs=[
            whole(D // BLOCK, TOKENS, BLOCK),
            whole(TOKENS, BLOCK),
            pl.BlockSpec((1, WIDTH), lambda i: (0, i)),
            pl.BlockSpec((ROWS, WIDTH), lambda i: (0, i)),
            whole(ROWS, masks.shape[1]),
            pl.BlockSpec((PER_STEP, BLOCK, BLOCK), lambda i: (i, 0, 0)),
        ],
        out_specs=[whole(TOKENS, ROWS), pl.BlockSpec((ROWS, WIDTH), lambda i: (0, i))],
        out_shape=[
            jax.ShapeDtypeStruct((TOKENS, ROWS), BF),
            jax.ShapeDtypeStruct((ROWS, D), BF),
        ],
        scratch_shapes=[pltpu.VMEM((TOKENS, BLOCK), F32), pltpu.VMEM((TOKENS, ROWS), F32)],
        name="refit",
    )(x, own, gain, weights, masks, inverse)


def to_next(section, shift):
    return [
        (section * Y * Z + y * Z + z, (section + 1) * Y * Z + ((y + shift) % Y) * Z + z)
        for y in range(Y)
        for z in range(Z)
    ]


def body(stream_in, gains, weights, masks, inv_hessian):
    section = lax.axis_index("section")
    y = lax.axis_index("dp") // Z
    rows = weights[0]
    mask_rows = masks[0]
    inverse = lax.all_gather(inv_hessian[0].astype(BF), "dp", axis=0, tiled=True)

    kept = keep_weights(rows, mask_rows)
    kept = lax.all_to_all(kept, "dp", 0, 0, axis_index_groups=Y_GROUPS)
    kept = lax.dynamic_slice_in_dim(jnp.concatenate([kept, kept], axis=0), y, Y, 0)
    kept = kept.reshape(Y * ROWS, SPAN)
    gain = lax.dynamic_slice_in_dim(gains, y * SPAN, SPAN, 1)

    own = stream_in
    mine = jnp.zeros((Z, TOKENS, BLOCK), BF)
    my_own = own
    for phase in range(SECTIONS):
        spread_own = jnp.broadcast_to(own[None], (Z, TOKENS, BLOCK))
        x = lax.all_to_all(spread_own, "dp", 0, 0, axis_index_groups=Z_GROUPS)
        here = section == phase
        mine = jnp.where(here, x, mine)
        my_own = jnp.where(here, own, my_own)
        if phase == SECTIONS - 1:
            break
        messages = layer(x, own, gain, kept)
        own = join(
            [lax.ppermute(m, AXES, to_next(phase, k)) for k, m in enumerate(messages)]
        )

    mine = jnp.broadcast_to(mine[None], (Y, Z, TOKENS, BLOCK))
    x = lax.all_to_all(mine, "dp", 0, 0, axis_index_groups=Y_GROUPS)
    x = x.reshape(Y * Z, TOKENS, BLOCK)
    stream, refitted = refit(x, my_own, gains, rows, mask_rows, inverse)
    return (stream[None], refitted[None])


def solution(mesh):
    placed = (
        P(None, "dp"),
        P("section", None),
        P("section", "dp", None),
        P("section", "dp", None),
        P("section", "dp", None, None),
    )
    return jax.shard_map(
        body,
        mesh=mesh,
        in_specs=placed,
        out_specs=(P("section", None, "dp"), P("section", "dp", None)),
        check_vma=False,
    )
```

```python
import functools

import jax
import jax.numpy as jnp
from jax import lax
from jax.experimental import pallas as pl
from jax.experimental.pallas import tpu as pltpu
from jax.sharding import PartitionSpec as P

D = 8192
BLOCK = 128
HALF = BLOCK // 2
ROWS = 128
TOKENS = 128
Y = 4
Z = 16
SECTIONS = 8
SPAN = Z * BLOCK
SCALE = D ** (-0.5)
EPS = 1e-05
AXES = ("section", "dp")
Y_GROUPS = [[y * Z + z for y in range(Y)] for z in range(Z)]
Z_GROUPS = [[y * Z + z for z in range(Z)] for y in range(Y)]
BF = jnp.bfloat16
F32 = jnp.float32
NT = (((1,), (1,)), ((), ()))
TN = (((0,), (0,)), ((), ()))
SMALL = pltpu.CompilerParams(vmem_limit_bytes=24 << 20)


def spread(masks, first, width):
    column = lax.broadcasted_iota(jnp.int32, (masks.shape[1], width), 1) + first
    row = lax.broadcasted_iota(jnp.int32, (masks.shape[1], width), 0)
    low = row * HALF
    chosen = ((column >= low) & (column < low + HALF)).astype(F32).astype(BF)
    return jnp.dot(masks.astype(F32).astype(BF), chosen, preferred_element_type=F32)


def keep_kernel(place_ref, weights_ref, masks_ref, kept_ref):
    width = weights_ref.shape[1]
    keep = spread(masks_ref[...], place_ref[0] * width, width)
    kept_ref[...] = (weights_ref[...].astype(F32) * keep).astype(BF)


def keep_weights(place, weights, masks):
    return pl.pallas_call(
        keep_kernel,
        grid_spec=pltpu.PrefetchScalarGridSpec(
            num_scalar_prefetch=1,
            grid=(1,),
            in_specs=[
                pl.BlockSpec((ROWS, SPAN), lambda i, place: (0, place[0])),
                pl.BlockSpec((ROWS, masks.shape[1]), lambda i, place: (0, 0)),
            ],
            out_specs=pl.BlockSpec((ROWS, SPAN), lambda i, place: (0, 0)),
        ),
        out_shape=jax.ShapeDtypeStruct((ROWS, SPAN), BF),
        compiler_params=SMALL,
        name="keep_weights",
    )(place.reshape(1), weights, masks)


def layer_kernel(x_ref, own_ref, gain_ref, *refs):
    kept_refs, outs, scaled = refs[:Y], refs[Y : 2 * Y], refs[2 * Y]
    squares = jnp.zeros((TOKENS, BLOCK), F32)
    for j in range(Z):
        x = x_ref[j].astype(F32)
        squares = squares + x * x
        scaled[:, j * BLOCK : (j + 1) * BLOCK] = (
            x * gain_ref[:, j * BLOCK : (j + 1) * BLOCK]
        ).astype(BF)
    total = jnp.sum(squares, axis=1, keepdims=True)
    high = total.astype(BF)
    low = (total - high.astype(F32)).astype(BF)
    lane = lax.broadcasted_iota(jnp.int32, (TOKENS, BLOCK), 1)
    both = jnp.where(
        lane < HALF,
        jnp.broadcast_to(high.astype(F32), (TOKENS, BLOCK)),
        jnp.broadcast_to(low.astype(F32), (TOKENS, BLOCK)),
    ).astype(BF)
    for k in range(Y):
        partial = lax.dot_general(
            scaled[...], kept_refs[k][...], NT, preferred_element_type=F32
        )
        outs[k][:, :BLOCK] = (partial * SCALE).astype(BF)
        outs[k][:, BLOCK : 2 * BLOCK] = both
    outs[0][:, 2 * BLOCK :] = own_ref[...]


def layer(x, own, gain, kept):
    widths = [3 * BLOCK] + [2 * BLOCK] * (Y - 1)
    return pl.pallas_call(
        layer_kernel,
        out_shape=[jax.ShapeDtypeStruct((TOKENS, w), BF) for w in widths],
        scratch_shapes=[pltpu.VMEM((TOKENS, SPAN), BF)],
        compiler_params=SMALL,
        name="layer",
    )(x, own, gain, *kept)


def join(parts):
    projected = sum(p[:, :BLOCK].astype(F32) for p in parts)
    total = sum(
        p[:, BLOCK : BLOCK + 1].astype(F32) + p[:, BLOCK + HALF : BLOCK + HALF + 1].astype(F32)
        for p in parts
    )
    inverse = lax.rsqrt(total * (1.0 / D) + EPS)
    return (parts[0][:, 2 * BLOCK :].astype(F32) + projected * inverse).astype(BF)


PER_STEP = 8
WIDTH = PER_STEP * BLOCK


def refit_kernel(x_ref, own_ref, gain_ref, weights_ref, masks_ref, inverse_ref, stream_ref, refit_ref, norm, acc):
    step = pl.program_id(0)

    @pl.when(step == 0)
    def _():
        def add(b, squares):
            x = x_ref[b].astype(F32)
            return squares + x * x

        squares = lax.fori_loop(0, D // BLOCK, add, jnp.zeros((TOKENS, BLOCK), F32), unroll=8)
        total = jnp.sum(squares, axis=1, keepdims=True)
        norm[...] = jnp.broadcast_to(lax.rsqrt(total * (1.0 / D) + EPS), (TOKENS, BLOCK))
        acc[...] = jnp.zeros((TOKENS, ROWS), F32)

    keep = spread(masks_ref[...], step * WIDTH, WIDTH)
    scale = norm[...]
    projected = acc[...]
    for j in range(PER_STEP):
        cut = slice(j * BLOCK, (j + 1) * BLOCK)
        x = x_ref[step * PER_STEP + j].astype(F32)
        normed = (x * scale * gain_ref[:, cut]).astype(BF)
        gram = lax.dot_general(normed, normed, TN, preferred_element_type=F32)
        hessian = (gram * (1.0 / TOKENS)).astype(BF)
        product = jnp.dot(hessian, inverse_ref[j], preferred_element_type=F32).astype(BF)
        weights = weights_ref[:, cut].astype(F32)
        kept = weights * keep[:, cut]
        removed = (weights - kept).astype(BF)
        update = jnp.dot(removed, product, preferred_element_type=F32)
        refit_ref[:, cut] = (keep[:, cut] * (weights + update)).astype(BF)
        projected = projected + lax.dot_general(
            normed, kept.astype(BF), NT, preferred_element_type=F32
        )
    acc[...] = projected

    @pl.when(step == D // WIDTH - 1)
    def _():
        stream_ref[...] = (own_ref[...].astype(F32) + projected * SCALE).astype(BF)


def refit(x, own, gain, weights, masks, inverse):
    whole = lambda *shape: pl.BlockSpec(shape, lambda i: (0,) * len(shape))
    return pl.pallas_call(
        refit_kernel,
        grid=(D // WIDTH,),
        in_specs=[
            whole(D // BLOCK, TOKENS, BLOCK),
            whole(TOKENS, BLOCK),
            pl.BlockSpec((1, WIDTH), lambda i: (0, i)),
            pl.BlockSpec((ROWS, WIDTH), lambda i: (0, i)),
            whole(ROWS, masks.shape[1]),
            pl.BlockSpec((PER_STEP, BLOCK, BLOCK), lambda i: (i, 0, 0)),
        ],
        out_specs=[whole(TOKENS, ROWS), pl.BlockSpec((ROWS, WIDTH), lambda i: (0, i))],
        out_shape=[
            jax.ShapeDtypeStruct((TOKENS, ROWS), BF),
            jax.ShapeDtypeStruct((ROWS, D), BF),
        ],
        scratch_shapes=[pltpu.VMEM((TOKENS, BLOCK), F32), pltpu.VMEM((TOKENS, ROWS), F32)],
        compiler_params=SMALL,
        name="refit",
    )(x, own, gain, weights, masks, inverse)


def to_next(section, shift):
    return [
        (section * Y * Z + y * Z + z, (section + 1) * Y * Z + ((y + shift) % Y) * Z + z)
        for y in range(Y)
        for z in range(Z)
    ]


def along_y(shift):
    return [
        (s * Y * Z + y * Z + z, s * Y * Z + ((y + shift) % Y) * Z + z)
        for s in range(SECTIONS)
        for y in range(Y)
        for z in range(Z)
    ]


def body(stream_in, gains, weights, masks, inv_hessian):
    section = lax.axis_index("section")
    y = lax.axis_index("dp") // Z
    rows = weights[0]
    mask_rows = masks[0]
    inverse_own = inv_hessian[0, 0].astype(BF)

    def gather_y(blocks):
        copies = jnp.broadcast_to(blocks[None], (Y,) + blocks.shape)
        got = lax.all_to_all(copies, "dp", 0, 0, axis_index_groups=Y_GROUPS)
        return got.reshape((Y * Z,) + blocks.shape[1:])

    def gather_z(own):
        copies = jnp.broadcast_to(own[None], (Z, TOKENS, BLOCK))
        return lax.all_to_all(copies, "dp", 0, 0, axis_index_groups=Z_GROUPS)

    kept = [keep_weights(lax.rem(y + k, Y), rows, mask_rows) for k in range(Y)]
    kept = [kept[0]] + [
        lax.ppermute(kept[Y - k], AXES, along_y(Y - k)) for k in range(1, Y)
    ]
    gain = lax.dynamic_slice_in_dim(gains, y * SPAN, SPAN, 1)

    own = stream_in
    mine = lax.cond(
        section != 1,
        gather_z,
        lambda o: jnp.zeros((Z, TOKENS, BLOCK), BF),
        jnp.where(section == 0, own, inverse_own),
    )
    inverse_z = mine
    my_own = own
    inverse = jnp.zeros((Y * Z, BLOCK, BLOCK), BF)
    widths = [3 * BLOCK] + [2 * BLOCK] * (Y - 1)
    for phase in range(SECTIONS - 1):
        here = section == phase

        def active(mine, own, *kept):
            x = gather_z(own) if phase else mine
            return [x, *layer(x, own, gain, kept)]

        def idle(mine, own, *kept):
            return [mine] + [jnp.zeros((TOKENS, w), BF) for w in widths]

        mine, *messages = lax.cond(here, active, idle, mine, own, *kept)
        my_own = jnp.where(here, own, my_own)
        parts = [lax.ppermute(m, AXES, to_next(phase, k)) for k, m in enumerate(messages)]
        if phase == 0:
            messages, inverse_z = lax.optimization_barrier((messages, inverse_z))
            inverse = lax.cond(section >= 2, lambda z, i: gather_y(z), lambda z, i: i, inverse_z, inverse)
            parts, inverse = lax.optimization_barrier((parts, inverse))
        if phase == 2:
            messages, inverse_own = lax.optimization_barrier((messages, inverse_own))
            inverse = lax.cond(
                section < 2, lambda b, i: gather_y(gather_z(b)), lambda b, i: i, inverse_own, inverse
            )
            parts, inverse = lax.optimization_barrier((parts, inverse))
        own = join(parts)

    last = section == SECTIONS - 1
    mine = lax.cond(last, lambda m, o: gather_z(o), lambda m, o: m, mine, own)
    my_own = jnp.where(last, own, my_own)
    x = gather_y(mine)
    stream, refitted = refit(x, my_own, gains, rows, mask_rows, inverse)
    return (stream[None], refitted[None])


def solution(mesh):
    placed = (
        P(None, "dp"),
        P("section", None),
        P("section", "dp", None),
        P("section", "dp", None),
        P("section", "dp", None, None),
    )
    return jax.shard_map(
        body,
        mesh=mesh,
        in_specs=placed,
        out_specs=(P("section", None, "dp"), P("section", "dp", None)),
        check_vma=False,
    )
```

```python
import functools

import jax
import jax.numpy as jnp
from jax import lax
from jax.experimental import pallas as pl
from jax.experimental.pallas import tpu as pltpu
from jax.sharding import PartitionSpec as P

D = 8192
BLOCK = 128
HALF = BLOCK // 2
ROWS = 128
TOKENS = 128
Y = 4
Z = 16
SECTIONS = 8
SPAN = Z * BLOCK
SCALE = D ** (-0.5)
EPS = 1e-05
AXES = ("section", "dp")
Y_GROUPS = [[y * Z + z for y in range(Y)] for z in range(Z)]
Z_GROUPS = [[y * Z + z for z in range(Z)] for y in range(Y)]
BF = jnp.bfloat16
F32 = jnp.float32
NT = (((1,), (1,)), ((), ()))
TN = (((0,), (0,)), ((), ()))
SMALL = pltpu.CompilerParams(vmem_limit_bytes=24 << 20)


def spread(masks, first, width):
    column = lax.broadcasted_iota(jnp.int32, (masks.shape[1], width), 1) + first
    row = lax.broadcasted_iota(jnp.int32, (masks.shape[1], width), 0)
    low = row * HALF
    chosen = ((column >= low) & (column < low + HALF)).astype(F32).astype(BF)
    return jnp.dot(masks.astype(F32).astype(BF), chosen, preferred_element_type=F32)


def keep_kernel(place_ref, weights_ref, masks_ref, kept_ref):
    width = weights_ref.shape[1]
    keep = spread(masks_ref[...], place_ref[0] * width, width)
    kept_ref[...] = (weights_ref[...].astype(F32) * keep).astype(BF)


def keep_weights(place, weights, masks):
    return pl.pallas_call(
        keep_kernel,
        grid_spec=pltpu.PrefetchScalarGridSpec(
            num_scalar_prefetch=1,
            grid=(1,),
            in_specs=[
                pl.BlockSpec((ROWS, SPAN), lambda i, place: (0, place[0])),
                pl.BlockSpec((ROWS, masks.shape[1]), lambda i, place: (0, 0)),
            ],
            out_specs=pl.BlockSpec((ROWS, SPAN), lambda i, place: (0, 0)),
        ),
        out_shape=jax.ShapeDtypeStruct((ROWS, SPAN), BF),
        compiler_params=SMALL,
        name="keep_weights",
    )(place.reshape(1), weights, masks)


def layer_kernel(x_ref, own_ref, gain_ref, *refs):
    kept_refs, outs, scaled = refs[:Y], refs[Y : 2 * Y], refs[2 * Y]
    squares = jnp.zeros((TOKENS, BLOCK), F32)
    for j in range(Z):
        x = x_ref[j].astype(F32)
        squares = squares + x * x
        scaled[:, j * BLOCK : (j + 1) * BLOCK] = (
            x * gain_ref[:, j * BLOCK : (j + 1) * BLOCK]
        ).astype(BF)
    total = jnp.sum(squares, axis=1, keepdims=True)
    high = total.astype(BF)
    low = (total - high.astype(F32)).astype(BF)
    lane = lax.broadcasted_iota(jnp.int32, (TOKENS, BLOCK), 1)
    both = jnp.where(
        lane < HALF,
        jnp.broadcast_to(high.astype(F32), (TOKENS, BLOCK)),
        jnp.broadcast_to(low.astype(F32), (TOKENS, BLOCK)),
    ).astype(BF)
    for k in range(Y):
        partial = lax.dot_general(
            scaled[...], kept_refs[k][...], NT, preferred_element_type=F32
        )
        outs[k][:, :BLOCK] = (partial * SCALE).astype(BF)
        outs[k][:, BLOCK : 2 * BLOCK] = both
    outs[0][:, 2 * BLOCK :] = own_ref[...]


def layer(x, own, gain, kept):
    widths = [3 * BLOCK] + [2 * BLOCK] * (Y - 1)
    return pl.pallas_call(
        layer_kernel,
        out_shape=[jax.ShapeDtypeStruct((TOKENS, w), BF) for w in widths],
        scratch_shapes=[pltpu.VMEM((TOKENS, SPAN), BF)],
        compiler_params=SMALL,
        name="layer",
    )(x, own, gain, *kept)


def join(parts):
    projected = sum(p[:, :BLOCK].astype(F32) for p in parts)
    total = sum(
        p[:, BLOCK : BLOCK + 1].astype(F32) + p[:, BLOCK + HALF : BLOCK + HALF + 1].astype(F32)
        for p in parts
    )
    inverse = lax.rsqrt(total * (1.0 / D) + EPS)
    return (parts[0][:, 2 * BLOCK :].astype(F32) + projected * inverse).astype(BF)


def mask_kernel(masks_ref, keep_ref):
    width = keep_ref.shape[1]
    keep_ref[...] = spread(masks_ref[...], pl.program_id(0) * width, width).astype(BF)


def spread_masks(masks):
    return pl.pallas_call(
        mask_kernel,
        grid=(Y,),
        in_specs=[pl.BlockSpec((ROWS, masks.shape[1]), lambda i: (0, 0))],
        out_specs=pl.BlockSpec((ROWS, SPAN), lambda i: (0, i)),
        out_shape=jax.ShapeDtypeStruct((ROWS, D), BF),
        compiler_params=SMALL,
        name="spread_masks",
    )(masks)


PER_STEP = 16
WIDTH = PER_STEP * BLOCK


def refit_kernel(
    x_ref, own_ref, gain_ref, weights_ref, keep_ref, inverse_ref, stream_ref, refit_ref,
    norm, acc, normed, met, turned,
):
    step = pl.program_id(0)

    @pl.when(step == 0)
    def _():
        def add(b, squares):
            x = x_ref[b].astype(F32)
            return squares + x * x

        squares = lax.fori_loop(0, D // BLOCK, add, jnp.zeros((TOKENS, BLOCK), F32), unroll=8)
        total = jnp.sum(squares, axis=1, keepdims=True)
        norm[...] = jnp.broadcast_to(lax.rsqrt(total * (1.0 / D) + EPS), (TOKENS, BLOCK))
        acc[...] = jnp.zeros((TOKENS, ROWS), F32)

    scale = norm[...]
    cuts = [slice(j * BLOCK, (j + 1) * BLOCK) for j in range(PER_STEP)]
    for j, cut in enumerate(cuts):
        x = x_ref[step * PER_STEP + j].astype(F32)
        normed[:, cut] = (x * scale * gain_ref[:, cut]).astype(BF)
    weights = weights_ref[...]
    keep = keep_ref[...]
    kept = weights * keep
    removed = weights - kept
    acc[...] += lax.dot_general(normed[...], kept, NT, preferred_element_type=F32)
    for j, cut in enumerate(cuts):
        product = lax.dot_general(
            removed[:, cut], normed[:, cut], NT, preferred_element_type=F32
        )
        met[:, cut] = (product * (1.0 / TOKENS)).astype(BF)
        turned[:, cut] = jnp.dot(
            normed[:, cut], inverse_ref[j], preferred_element_type=F32
        ).astype(BF)
    for cut in cuts:
        update = jnp.dot(met[:, cut], turned[:, cut], preferred_element_type=F32)
        refit_ref[:, cut] = (
            keep[:, cut].astype(F32) * (weights[:, cut].astype(F32) + update)
        ).astype(BF)

    @pl.when(step == D // WIDTH - 1)
    def _():
        stream_ref[...] = (own_ref[...].astype(F32) + acc[...] * SCALE).astype(BF)


def refit(x, own, gain, weights, keep, inverse):
    whole = lambda *shape: pl.BlockSpec(shape, lambda i: (0,) * len(shape))
    cut = lambda rows: pl.BlockSpec((rows, WIDTH), lambda i: (0, i))
    return pl.pallas_call(
        refit_kernel,
        grid=(D // WIDTH,),
        in_specs=[
            whole(D // BLOCK, TOKENS, BLOCK),
            whole(TOKENS, BLOCK),
            cut(1),
            cut(ROWS),
            cut(ROWS),
            pl.BlockSpec((PER_STEP, BLOCK, BLOCK), lambda i: (i, 0, 0)),
        ],
        out_specs=[whole(TOKENS, ROWS), cut(ROWS)],
        out_shape=[
            jax.ShapeDtypeStruct((TOKENS, ROWS), BF),
            jax.ShapeDtypeStruct((ROWS, D), BF),
        ],
        scratch_shapes=[pltpu.VMEM((TOKENS, BLOCK), F32), pltpu.VMEM((TOKENS, ROWS), F32)]
        + [pltpu.VMEM((ROWS, WIDTH), BF)] * 3,
        compiler_params=SMALL,
        name="refit",
    )(x, own, gain, weights, keep, inverse)


def to_next(section, shift):
    return [
        (section * Y * Z + y * Z + z, (section + 1) * Y * Z + ((y + shift) % Y) * Z + z)
        for y in range(Y)
        for z in range(Z)
    ]


def along_y(shift):
    return [
        (s * Y * Z + y * Z + z, s * Y * Z + ((y + shift) % Y) * Z + z)
        for s in range(SECTIONS)
        for y in range(Y)
        for z in range(Z)
    ]


def body(stream_in, gains, weights, masks, inv_hessian):
    section = lax.axis_index("section")
    y = lax.axis_index("dp") // Z
    rows = weights[0]
    mask_rows = masks[0]
    inverse_own = inv_hessian[0, 0].astype(BF)

    def gather_y(blocks):
        copies = jnp.broadcast_to(blocks[None], (Y,) + blocks.shape)
        got = lax.all_to_all(copies, "dp", 0, 0, axis_index_groups=Y_GROUPS)
        return got.reshape((Y * Z,) + blocks.shape[1:])

    def gather_z(own):
        copies = jnp.broadcast_to(own[None], (Z, TOKENS, BLOCK))
        return lax.all_to_all(copies, "dp", 0, 0, axis_index_groups=Z_GROUPS)

    kept = [keep_weights(lax.rem(y + k, Y), rows, mask_rows) for k in range(Y)]
    kept = [kept[0]] + [
        lax.ppermute(kept[Y - k], AXES, along_y(Y - k)) for k in range(1, Y)
    ]
    gain = lax.dynamic_slice_in_dim(gains, y * SPAN, SPAN, 1)

    own = stream_in
    mine = lax.cond(
        section != 1,
        gather_z,
        lambda o: jnp.zeros((Z, TOKENS, BLOCK), BF),
        jnp.where(section == 0, own, inverse_own),
    )
    inverse_z = mine
    my_own = own
    inverse = jnp.zeros((Y * Z, BLOCK, BLOCK), BF)
    widths = [3 * BLOCK] + [2 * BLOCK] * (Y - 1)
    for phase in range(SECTIONS - 1):
        here = section == phase

        def active(mine, own, *kept):
            x = gather_z(own) if phase else mine
            return [x, *layer(x, own, gain, kept)]

        def idle(mine, own, *kept):
            return [mine] + [jnp.zeros((TOKENS, w), BF) for w in widths]

        mine, *messages = lax.cond(here, active, idle, mine, own, *kept)
        my_own = jnp.where(here, own, my_own)
        parts = [lax.ppermute(m, AXES, to_next(phase, k)) for k, m in enumerate(messages)]
        if phase == 0:
            messages, inverse_z = lax.optimization_barrier((messages, inverse_z))
            inverse = lax.cond(section >= 2, lambda z, i: gather_y(z), lambda z, i: i, inverse_z, inverse)
            parts, inverse = lax.optimization_barrier((parts, inverse))
        if phase == 1:
            messages, mask_rows = lax.optimization_barrier((messages, mask_rows))
            keep = spread_masks(mask_rows)
            parts, keep = lax.optimization_barrier((parts, keep))
        if phase == 2:
            messages, inverse_own = lax.optimization_barrier((messages, inverse_own))
            inverse = lax.cond(
                section < 2, lambda b, i: gather_y(gather_z(b)), lambda b, i: i, inverse_own, inverse
            )
            parts, inverse = lax.optimization_barrier((parts, inverse))
        own = join(parts)

    last = section == SECTIONS - 1
    mine = lax.cond(last, lambda m, o: gather_z(o), lambda m, o: m, mine, own)
    my_own = jnp.where(last, own, my_own)
    x = gather_y(mine)
    stream, refitted = refit(x, my_own, gains, rows, keep, inverse)
    return (stream[None], refitted[None])


def solution(mesh):
    placed = (
        P(None, "dp"),
        P("section", None),
        P("section", "dp", None),
        P("section", "dp", None),
        P("section", "dp", None, None),
    )
    return jax.shard_map(
        body,
        mesh=mesh,
        in_specs=placed,
        out_specs=(P("section", None, "dp"), P("section", "dp", None)),
        check_vma=False,
    )
```

```python
import functools

import jax
import jax.numpy as jnp
from jax import lax
from jax.experimental import pallas as pl
from jax.experimental.pallas import tpu as pltpu
from jax.sharding import PartitionSpec as P

D = 8192
BLOCK = 128
HALF = BLOCK // 2
ROWS = 128
TOKENS = 128
Y = 4
Z = 16
SECTIONS = 8
SPAN = Z * BLOCK
SCALE = D ** (-0.5)
EPS = 1e-05
AXES = ("section", "dp")
Y_GROUPS = [[y * Z + z for y in range(Y)] for z in range(Z)]
Z_GROUPS = [[y * Z + z for z in range(Z)] for y in range(Y)]
BF = jnp.bfloat16
F32 = jnp.float32
NT = (((1,), (1,)), ((), ()))
TN = (((0,), (0,)), ((), ()))
SMALL = pltpu.CompilerParams(vmem_limit_bytes=24 << 20)


def spread(masks, first, width):
    column = lax.broadcasted_iota(jnp.int32, (masks.shape[1], width), 1) + first
    row = lax.broadcasted_iota(jnp.int32, (masks.shape[1], width), 0)
    low = row * HALF
    chosen = ((column >= low) & (column < low + HALF)).astype(F32).astype(BF)
    return jnp.dot(masks.astype(F32).astype(BF), chosen, preferred_element_type=F32)


def keep_kernel(place_ref, weights_ref, masks_ref, kept_ref):
    width = weights_ref.shape[1]
    keep = spread(masks_ref[...], place_ref[0] * width, width)
    kept_ref[...] = (weights_ref[...].astype(F32) * keep).astype(BF)


def keep_weights(place, weights, masks):
    return pl.pallas_call(
        keep_kernel,
        grid_spec=pltpu.PrefetchScalarGridSpec(
            num_scalar_prefetch=1,
            grid=(1,),
            in_specs=[
                pl.BlockSpec((ROWS, SPAN), lambda i, place: (0, place[0])),
                pl.BlockSpec((ROWS, masks.shape[1]), lambda i, place: (0, 0)),
            ],
            out_specs=pl.BlockSpec((ROWS, SPAN), lambda i, place: (0, 0)),
        ),
        out_shape=jax.ShapeDtypeStruct((ROWS, SPAN), BF),
        compiler_params=SMALL,
        name="keep_weights",
    )(place.reshape(1), weights, masks)


def layer_kernel(x_ref, own_ref, gain_ref, *refs):
    kept_refs, outs, scaled = refs[:Y], refs[Y : 2 * Y], refs[2 * Y]
    squares = jnp.zeros((TOKENS, BLOCK), F32)
    for j in range(Z):
        x = x_ref[j].astype(F32)
        squares = squares + x * x
        scaled[:, j * BLOCK : (j + 1) * BLOCK] = (
            x * gain_ref[:, j * BLOCK : (j + 1) * BLOCK]
        ).astype(BF)
    total = jnp.sum(squares, axis=1, keepdims=True)
    high = total.astype(BF)
    low = (total - high.astype(F32)).astype(BF)
    lane = lax.broadcasted_iota(jnp.int32, (TOKENS, BLOCK), 1)
    both = jnp.where(
        lane < HALF,
        jnp.broadcast_to(high.astype(F32), (TOKENS, BLOCK)),
        jnp.broadcast_to(low.astype(F32), (TOKENS, BLOCK)),
    ).astype(BF)
    for k in range(Y):
        partial = lax.dot_general(
            scaled[...], kept_refs[k][...], NT, preferred_element_type=F32
        )
        outs[k][:, :BLOCK] = (partial * SCALE).astype(BF)
        outs[k][:, BLOCK : 2 * BLOCK] = both
    outs[0][:, 2 * BLOCK :] = own_ref[...]


def layer(x, own, gain, kept):
    widths = [3 * BLOCK] + [2 * BLOCK] * (Y - 1)
    return pl.pallas_call(
        layer_kernel,
        out_shape=[jax.ShapeDtypeStruct((TOKENS, w), BF) for w in widths],
        scratch_shapes=[pltpu.VMEM((TOKENS, SPAN), BF)],
        compiler_params=SMALL,
        name="layer",
    )(x, own, gain, *kept)


def join(parts):
    projected = sum(p[:, :BLOCK].astype(F32) for p in parts)
    total = sum(
        p[:, BLOCK : BLOCK + 1].astype(F32) + p[:, BLOCK + HALF : BLOCK + HALF + 1].astype(F32)
        for p in parts
    )
    inverse = lax.rsqrt(total * (1.0 / D) + EPS)
    return (parts[0][:, 2 * BLOCK :].astype(F32) + projected * inverse).astype(BF)


def mask_kernel(masks_ref, keep_ref):
    width = keep_ref.shape[1]
    keep_ref[...] = spread(masks_ref[...], pl.program_id(0) * width, width).astype(BF)


def spread_masks(masks):
    return pl.pallas_call(
        mask_kernel,
        grid=(Y,),
        in_specs=[pl.BlockSpec((ROWS, masks.shape[1]), lambda i: (0, 0))],
        out_specs=pl.BlockSpec((ROWS, SPAN), lambda i: (0, i)),
        out_shape=jax.ShapeDtypeStruct((ROWS, D), BF),
        compiler_params=SMALL,
        name="spread_masks",
    )(masks)


PER_STEP = 16
WIDTH = PER_STEP * BLOCK


def refit_kernel(
    x_ref, own_ref, gain_ref, weights_ref, keep_ref, inverse_ref, stream_ref, refit_ref,
    norm, acc, normed, met, turned,
):
    step = pl.program_id(0)

    @pl.when(step == 0)
    def _():
        def add(b, squares):
            x = x_ref[b].astype(F32)
            return squares + x * x

        squares = lax.fori_loop(0, D // BLOCK, add, jnp.zeros((TOKENS, BLOCK), F32), unroll=8)
        total = jnp.sum(squares, axis=1, keepdims=True)
        norm[...] = jnp.broadcast_to(lax.rsqrt(total * (1.0 / D) + EPS), (TOKENS, BLOCK))
        acc[...] = jnp.zeros((TOKENS, ROWS), F32)

    scale = norm[...]
    cuts = [slice(j * BLOCK, (j + 1) * BLOCK) for j in range(PER_STEP)]
    for j, cut in enumerate(cuts):
        x = x_ref[step * PER_STEP + j].astype(F32)
        normed[:, cut] = (x * scale * gain_ref[:, cut]).astype(BF)
    weights = weights_ref[...]
    keep = keep_ref[...]
    kept = weights * keep
    removed = weights - kept
    acc[...] += lax.dot_general(normed[...], kept, NT, preferred_element_type=F32)
    for j, cut in enumerate(cuts):
        product = lax.dot_general(
            removed[:, cut], normed[:, cut], NT, preferred_element_type=F32
        )
        met[:, cut] = (product * (1.0 / TOKENS)).astype(BF)
        turned[:, cut] = jnp.dot(
            normed[:, cut], inverse_ref[j], preferred_element_type=F32
        ).astype(BF)
    for cut in cuts:
        update = jnp.dot(met[:, cut], turned[:, cut], preferred_element_type=F32)
        refit_ref[:, cut] = (
            keep[:, cut].astype(F32) * (weights[:, cut].astype(F32) + update)
        ).astype(BF)

    @pl.when(step == D // WIDTH - 1)
    def _():
        stream_ref[...] = (own_ref[...].astype(F32) + acc[...] * SCALE).astype(BF)


def refit(x, own, gain, weights, keep, inverse):
    whole = lambda *shape: pl.BlockSpec(shape, lambda i: (0,) * len(shape))
    cut = lambda rows: pl.BlockSpec((rows, WIDTH), lambda i: (0, i))
    return pl.pallas_call(
        refit_kernel,
        grid=(D // WIDTH,),
        in_specs=[
            whole(D // BLOCK, TOKENS, BLOCK),
            whole(TOKENS, BLOCK),
            cut(1),
            cut(ROWS),
            cut(ROWS),
            pl.BlockSpec((PER_STEP, BLOCK, BLOCK), lambda i: (i, 0, 0)),
        ],
        out_specs=[whole(TOKENS, ROWS), cut(ROWS)],
        out_shape=[
            jax.ShapeDtypeStruct((TOKENS, ROWS), BF),
            jax.ShapeDtypeStruct((ROWS, D), BF),
        ],
        scratch_shapes=[pltpu.VMEM((TOKENS, BLOCK), F32), pltpu.VMEM((TOKENS, ROWS), F32)]
        + [pltpu.VMEM((ROWS, WIDTH), BF)] * 3,
        compiler_params=SMALL,
        name="refit",
    )(x, own, gain, weights, keep, inverse)


def to_next(section, shift, answer):
    moves = [(section, section + 1)]
    if answer and section in (2, 4, 6):
        moves.append((section - 1, section - 2))
    return [
        (source * Y * Z + y * Z + z, target * Y * Z + ((y + shift) % Y) * Z + z)
        for source, target in moves
        for y in range(Y)
        for z in range(Z)
    ]


def along_y(shift):
    return [
        (s * Y * Z + y * Z + z, s * Y * Z + ((y + shift) % Y) * Z + z)
        for s in range(SECTIONS)
        for y in range(Y)
        for z in range(Z)
    ]


def body(stream_in, gains, weights, masks, inv_hessian):
    section = lax.axis_index("section")
    y = lax.axis_index("dp") // Z
    rows = weights[0]
    mask_rows = masks[0]
    inverse_own = inv_hessian[0, 0].astype(BF)

    def gather_y(blocks):
        copies = jnp.broadcast_to(blocks[None], (Y,) + blocks.shape)
        got = lax.all_to_all(copies, "dp", 0, 0, axis_index_groups=Y_GROUPS)
        return got.reshape((Y * Z,) + blocks.shape[1:])

    def gather_z(own):
        copies = jnp.broadcast_to(own[None], (Z, TOKENS, BLOCK))
        return lax.all_to_all(copies, "dp", 0, 0, axis_index_groups=Z_GROUPS)

    kept = [keep_weights(lax.rem(y + k, Y), rows, mask_rows) for k in range(Y)]
    kept = [kept[0]] + [
        lax.ppermute(kept[Y - k], AXES, along_y(Y - k)) for k in range(1, Y)
    ]
    gain = lax.dynamic_slice_in_dim(gains, y * SPAN, SPAN, 1)

    own = stream_in
    mine = lax.cond(
        (section == 0) | (section >= 4),
        gather_z,
        lambda o: jnp.zeros((Z, TOKENS, BLOCK), BF),
        jnp.where(section == 0, own, inverse_own),
    )
    inverse_z = mine
    my_own = own
    inverse = jnp.zeros((Y * Z, BLOCK, BLOCK), BF)
    widths = [3 * BLOCK] + [2 * BLOCK] * (Y - 1)
    for phase in range(SECTIONS - 1):
        here = section == phase

        def active(mine, own, *kept):
            x = gather_z(own) if phase else mine
            return [x, *layer(x, own, gain, kept)]

        def idle(mine, own, *kept):
            return [mine] + [jnp.zeros((TOKENS, w), BF) for w in widths]

        mine, *messages = lax.cond(here, active, idle, mine, own, *kept)
        my_own = jnp.where(here, own, my_own)
        parts = [lax.ppermute(m, AXES, to_next(phase, k, k == 0)) for k, m in enumerate(messages)]
        if phase == 0:
            messages, inverse_z = lax.optimization_barrier((messages, inverse_z))
            inverse = lax.cond(section >= 4, lambda z, i: gather_y(z), lambda z, i: i, inverse_z, inverse)
            parts, inverse = lax.optimization_barrier((parts, inverse))
        if phase == 1:
            messages, mask_rows = lax.optimization_barrier((messages, mask_rows))
            keep = spread_masks(mask_rows)
            parts, keep = lax.optimization_barrier((parts, keep))
        if phase in (3, 5):
            messages, inverse_own = lax.optimization_barrier((messages, inverse_own))
            inverse = lax.cond(
                (section == phase - 3) | (section == phase - 2), lambda b, i: gather_y(gather_z(b)), lambda b, i: i, inverse_own, inverse
            )
            parts, inverse = lax.optimization_barrier((parts, inverse))
        own = join(parts)

    last = section == SECTIONS - 1
    mine = lax.cond(last, lambda m, o: gather_z(o), lambda m, o: m, mine, own)
    my_own = jnp.where(last, own, my_own)
    x = gather_y(mine)
    stream, refitted = refit(x, my_own, gains, rows, keep, inverse)
    return (stream[None], refitted[None])


def solution(mesh):
    placed = (
        P(None, "dp"),
        P("section", None),
        P("section", "dp", None),
        P("section", "dp", None),
        P("section", "dp", None, None),
    )
    return jax.shard_map(
        body,
        mesh=mesh,
        in_specs=placed,
        out_specs=(P("section", None, "dp"), P("section", "dp", None)),
        check_vma=False,
    )
```

```python
import functools

import jax
import jax.numpy as jnp
from jax import lax
from jax.experimental import pallas as pl
from jax.experimental.pallas import tpu as pltpu
from jax.sharding import PartitionSpec as P

D = 8192
BLOCK = 128
HALF = BLOCK // 2
ROWS = 128
TOKENS = 128
Y = 4
Z = 16
SECTIONS = 8
SPAN = Z * BLOCK
SCALE = D ** (-0.5)
EPS = 1e-05
AXES = ("section", "dp")
Y_GROUPS = [[y * Z + z for y in range(Y)] for z in range(Z)]
Z_GROUPS = [[y * Z + z for z in range(Z)] for y in range(Y)]
BF = jnp.bfloat16
F32 = jnp.float32
NT = (((1,), (1,)), ((), ()))
TN = (((0,), (0,)), ((), ()))
SMALL = pltpu.CompilerParams(vmem_limit_bytes=24 << 20)


def spread(masks, first, width):
    column = lax.broadcasted_iota(jnp.int32, (masks.shape[1], width), 1) + first
    row = lax.broadcasted_iota(jnp.int32, (masks.shape[1], width), 0)
    low = row * HALF
    chosen = ((column >= low) & (column < low + HALF)).astype(F32).astype(BF)
    return jnp.dot(masks.astype(F32).astype(BF), chosen, preferred_element_type=F32)


def keep_kernel(place_ref, weights_ref, masks_ref, kept_ref):
    width = weights_ref.shape[1]
    keep = spread(masks_ref[...], place_ref[0] * width, width)
    kept_ref[...] = (weights_ref[...].astype(F32) * keep).astype(BF)


def keep_weights(place, weights, masks):
    return pl.pallas_call(
        keep_kernel,
        grid_spec=pltpu.PrefetchScalarGridSpec(
            num_scalar_prefetch=1,
            grid=(1,),
            in_specs=[
                pl.BlockSpec((ROWS, SPAN), lambda i, place: (0, place[0])),
                pl.BlockSpec((ROWS, masks.shape[1]), lambda i, place: (0, 0)),
            ],
            out_specs=pl.BlockSpec((ROWS, SPAN), lambda i, place: (0, 0)),
        ),
        out_shape=jax.ShapeDtypeStruct((ROWS, SPAN), BF),
        compiler_params=SMALL,
        name="keep_weights",
    )(place.reshape(1), weights, masks)


def layer_kernel(x_ref, own_ref, gain_ref, *refs):
    kept_refs, outs, scaled = refs[: -Y - 1], refs[-Y - 1 : -1], refs[-1]
    pieces = kept_refs if len(kept_refs) == Y else [kept_refs[0].at[k] for k in range(Y)]
    squares = jnp.zeros((TOKENS, BLOCK), F32)
    for j in range(Z):
        x = x_ref[j].astype(F32)
        squares = squares + x * x
        scaled[:, j * BLOCK : (j + 1) * BLOCK] = (
            x * gain_ref[:, j * BLOCK : (j + 1) * BLOCK]
        ).astype(BF)
    total = jnp.sum(squares, axis=1, keepdims=True)
    high = total.astype(BF)
    low = (total - high.astype(F32)).astype(BF)
    lane = lax.broadcasted_iota(jnp.int32, (TOKENS, BLOCK), 1)
    both = jnp.where(
        lane < HALF,
        jnp.broadcast_to(high.astype(F32), (TOKENS, BLOCK)),
        jnp.broadcast_to(low.astype(F32), (TOKENS, BLOCK)),
    ).astype(BF)
    for k in range(Y):
        partial = lax.dot_general(
            scaled[...], pieces[k][...], NT, preferred_element_type=F32
        )
        outs[k][:, :BLOCK] = (partial * SCALE).astype(BF)
        outs[k][:, BLOCK : 2 * BLOCK] = both
    outs[0][:, 2 * BLOCK :] = own_ref[...]


def layer(x, own, gain, kept):
    widths = [3 * BLOCK] + [2 * BLOCK] * (Y - 1)
    return pl.pallas_call(
        layer_kernel,
        out_shape=[jax.ShapeDtypeStruct((TOKENS, w), BF) for w in widths],
        scratch_shapes=[pltpu.VMEM((TOKENS, SPAN), BF)],
        compiler_params=SMALL,
        name="layer",
    )(x, own, gain, *kept)


def join(parts):
    projected = sum(p[:, :BLOCK].astype(F32) for p in parts)
    total = sum(
        p[:, BLOCK : BLOCK + 1].astype(F32) + p[:, BLOCK + HALF : BLOCK + HALF + 1].astype(F32)
        for p in parts
    )
    inverse = lax.rsqrt(total * (1.0 / D) + EPS)
    return (parts[0][:, 2 * BLOCK :].astype(F32) + projected * inverse).astype(BF)


def mask_kernel(masks_ref, keep_ref):
    width = keep_ref.shape[1]
    keep_ref[...] = spread(masks_ref[...], pl.program_id(0) * width, width).astype(BF)


def spread_masks(masks):
    return pl.pallas_call(
        mask_kernel,
        grid=(Y,),
        in_specs=[pl.BlockSpec((ROWS, masks.shape[1]), lambda i: (0, 0))],
        out_specs=pl.BlockSpec((ROWS, SPAN), lambda i: (0, i)),
        out_shape=jax.ShapeDtypeStruct((ROWS, D), BF),
        compiler_params=SMALL,
        name="spread_masks",
    )(masks)


PER_STEP = 16
WIDTH = PER_STEP * BLOCK


def refit_kernel(
    x_ref, own_ref, gain_ref, weights_ref, keep_ref, inverse_ref, stream_ref, refit_ref,
    norm, acc, normed, met, turned,
):
    step = pl.program_id(0)

    @pl.when(step == 0)
    def _():
        def add(b, squares):
            x = x_ref[b].astype(F32)
            return squares + x * x

        squares = lax.fori_loop(0, D // BLOCK, add, jnp.zeros((TOKENS, BLOCK), F32), unroll=8)
        total = jnp.sum(squares, axis=1, keepdims=True)
        norm[...] = jnp.broadcast_to(lax.rsqrt(total * (1.0 / D) + EPS), (TOKENS, BLOCK))
        acc[...] = jnp.zeros((TOKENS, ROWS), F32)

    scale = norm[...]
    cuts = [slice(j * BLOCK, (j + 1) * BLOCK) for j in range(PER_STEP)]
    for j, cut in enumerate(cuts):
        x = x_ref[step * PER_STEP + j].astype(F32)
        normed[:, cut] = (x * scale * gain_ref[:, cut]).astype(BF)
    weights = weights_ref[...]
    keep = keep_ref[...]
    kept = weights * keep
    removed = weights - kept
    acc[...] += lax.dot_general(normed[...], kept, NT, preferred_element_type=F32)
    for j, cut in enumerate(cuts):
        product = lax.dot_general(
            removed[:, cut], normed[:, cut], NT, preferred_element_type=F32
        )
        met[:, cut] = (product * (1.0 / TOKENS)).astype(BF)
        turned[:, cut] = jnp.dot(
            normed[:, cut], inverse_ref[j], preferred_element_type=F32
        ).astype(BF)
    for cut in cuts:
        update = jnp.dot(met[:, cut], turned[:, cut], preferred_element_type=F32)
        refit_ref[:, cut] = (
            keep[:, cut].astype(F32) * (weights[:, cut].astype(F32) + update)
        ).astype(BF)

    @pl.when(step == D // WIDTH - 1)
    def _():
        stream_ref[...] = (own_ref[...].astype(F32) + acc[...] * SCALE).astype(BF)


def refit(x, own, gain, weights, keep, inverse):
    whole = lambda *shape: pl.BlockSpec(shape, lambda i: (0,) * len(shape))
    cut = lambda rows: pl.BlockSpec((rows, WIDTH), lambda i: (0, i))
    return pl.pallas_call(
        refit_kernel,
        grid=(D // WIDTH,),
        in_specs=[
            whole(D // BLOCK, TOKENS, BLOCK),
            whole(TOKENS, BLOCK),
            cut(1),
            cut(ROWS),
            cut(ROWS),
            pl.BlockSpec((PER_STEP, BLOCK, BLOCK), lambda i: (i, 0, 0)),
        ],
        out_specs=[whole(TOKENS, ROWS), cut(ROWS)],
        out_shape=[
            jax.ShapeDtypeStruct((TOKENS, ROWS), BF),
            jax.ShapeDtypeStruct((ROWS, D), BF),
        ],
        scratch_shapes=[pltpu.VMEM((TOKENS, BLOCK), F32), pltpu.VMEM((TOKENS, ROWS), F32)]
        + [pltpu.VMEM((ROWS, WIDTH), BF)] * 3,
        compiler_params=SMALL,
        name="refit",
    )(x, own, gain, weights, keep, inverse)


def to_next(section, shift, answer):
    moves = [(section, section + 1)]
    if answer and section in (2, 4, 6):
        moves.append((section - 1, section - 2))
    return [
        (source * Y * Z + y * Z + z, target * Y * Z + ((y + shift) % Y) * Z + z)
        for source, target in moves
        for y in range(Y)
        for z in range(Z)
    ]


def along_y(shift):
    return [
        (s * Y * Z + y * Z + z, s * Y * Z + ((y + shift) % Y) * Z + z)
        for s in range(SECTIONS)
        for y in range(Y)
        for z in range(Z)
    ]


def body(stream_in, gains, weights, masks, inv_hessian):
    section = lax.axis_index("section")
    y = lax.axis_index("dp") // Z
    rows = weights[0]
    mask_rows = masks[0]
    inverse_own = inv_hessian[0, 0].astype(BF)

    def gather_y(blocks):
        copies = jnp.broadcast_to(blocks[None], (Y,) + blocks.shape)
        got = lax.all_to_all(copies, "dp", 0, 0, axis_index_groups=Y_GROUPS)
        return got.reshape((Y * Z,) + blocks.shape[1:])

    def gather_z(own):
        copies = jnp.broadcast_to(own[None], (Z, TOKENS, BLOCK))
        return lax.all_to_all(copies, "dp", 0, 0, axis_index_groups=Z_GROUPS)

    kept = [keep_weights(lax.rem(y + k, Y), rows, mask_rows) for k in range(Y)]
    kept = [kept[0]] + [
        lax.ppermute(kept[Y - k], AXES, along_y(Y - k)) for k in range(1, Y)
    ]
    gain = lax.dynamic_slice_in_dim(gains, y * SPAN, SPAN, 1)

    own = stream_in
    mine = lax.cond(
        (section == 0) | (section >= 4),
        gather_z,
        lambda o: jnp.zeros((Z, TOKENS, BLOCK), BF),
        jnp.where(section == 0, own, inverse_own),
    )
    inverse_z = mine
    my_own = own
    inverse = jnp.zeros((Y * Z, BLOCK, BLOCK), BF)
    widths = [3 * BLOCK] + [2 * BLOCK] * (Y - 1)
    for phase in range(SECTIONS - 1):
        here = section == phase

        def active(mine, own, *kept):
            x = gather_z(own) if phase else mine
            return [x, *layer(x, own, gain, kept)]

        def idle(mine, own, *kept):
            return [mine] + [jnp.zeros((TOKENS, w), BF) for w in widths]

        mine, *messages = lax.cond(here, active, idle, mine, own, *kept)
        my_own = jnp.where(here, own, my_own)
        parts = [lax.ppermute(m, AXES, to_next(phase, k, k == 0)) for k, m in enumerate(messages)]
        if phase == 0:
            messages, inverse_z, kept = lax.optimization_barrier((messages, inverse_z, kept))
            kept = [jnp.stack(kept)]
            inverse = lax.cond(section >= 4, lambda z, i: gather_y(z), lambda z, i: i, inverse_z, inverse)
            parts, inverse, kept = lax.optimization_barrier((parts, inverse, kept))
        if phase == 1:
            messages, mask_rows = lax.optimization_barrier((messages, mask_rows))
            keep = spread_masks(mask_rows)
            parts, keep = lax.optimization_barrier((parts, keep))
        if phase in (3, 5):
            messages, inverse_own = lax.optimization_barrier((messages, inverse_own))
            inverse = lax.cond(
                (section == phase - 3) | (section == phase - 2), lambda b, i: gather_y(gather_z(b)), lambda b, i: i, inverse_own, inverse
            )
            parts, inverse = lax.optimization_barrier((parts, inverse))
        own = join(parts)

    last = section == SECTIONS - 1
    mine = lax.cond(last, lambda m, o: gather_z(o), lambda m, o: m, mine, own)
    my_own = jnp.where(last, own, my_own)
    x = gather_y(mine)
    stream, refitted = refit(x, my_own, gains, rows, keep, inverse)
    return (stream[None], refitted[None])


def solution(mesh):
    placed = (
        P(None, "dp"),
        P("section", None),
        P("section", "dp", None),
        P("section", "dp", None),
        P("section", "dp", None, None),
    )
    return jax.shard_map(
        body,
        mesh=mesh,
        in_specs=placed,
        out_specs=(P("section", None, "dp"), P("section", "dp", None)),
        check_vma=False,
    )
```

```python
import functools

import jax
import jax.numpy as jnp
from jax import lax
from jax.experimental import pallas as pl
from jax.experimental.pallas import tpu as pltpu
from jax.sharding import PartitionSpec as P

D = 8192
BLOCK = 128
HALF = BLOCK // 2
ROWS = 128
TOKENS = 128
Y = 4
Z = 16
SECTIONS = 8
SPAN = Z * BLOCK
SCALE = D ** (-0.5)
SHIFTS = (2, 1, 3, 0)
EPS = 1e-05
AXES = ("section", "dp")
Y_GROUPS = [[y * Z + z for y in range(Y)] for z in range(Z)]
Z_GROUPS = [[y * Z + z for z in range(Z)] for y in range(Y)]
BF = jnp.bfloat16
F32 = jnp.float32
NT = (((1,), (1,)), ((), ()))
TN = (((0,), (0,)), ((), ()))
SMALL = pltpu.CompilerParams(vmem_limit_bytes=24 << 20)


def spread(masks, first, width):
    column = lax.broadcasted_iota(jnp.int32, (masks.shape[1], width), 1) + first
    row = lax.broadcasted_iota(jnp.int32, (masks.shape[1], width), 0)
    low = row * HALF
    chosen = ((column >= low) & (column < low + HALF)).astype(F32).astype(BF)
    return jnp.dot(masks.astype(F32).astype(BF), chosen, preferred_element_type=F32)


def keep_kernel(place_ref, weights_ref, masks_ref, kept_ref):
    width = weights_ref.shape[1]
    keep = spread(masks_ref[...], place_ref[0] * width, width)
    kept_ref[...] = (weights_ref[...].astype(F32) * keep).astype(BF)


def keep_weights(place, weights, masks):
    return pl.pallas_call(
        keep_kernel,
        grid_spec=pltpu.PrefetchScalarGridSpec(
            num_scalar_prefetch=1,
            grid=(1,),
            in_specs=[
                pl.BlockSpec((ROWS, SPAN), lambda i, place: (0, place[0])),
                pl.BlockSpec((ROWS, masks.shape[1]), lambda i, place: (0, 0)),
            ],
            out_specs=pl.BlockSpec((ROWS, SPAN), lambda i, place: (0, 0)),
        ),
        out_shape=jax.ShapeDtypeStruct((ROWS, SPAN), BF),
        compiler_params=SMALL,
        name="keep_weights",
    )(place.reshape(1), weights, masks)


def layer_kernel(x_ref, own_ref, gain_ref, *refs):
    kept_refs, outs, scaled = refs[:Y], refs[Y : 2 * Y], refs[2 * Y]
    squares = jnp.zeros((TOKENS, BLOCK), F32)
    for j in range(Z):
        x = x_ref[j].astype(F32)
        squares = squares + x * x
        scaled[:, j * BLOCK : (j + 1) * BLOCK] = (
            x * gain_ref[:, j * BLOCK : (j + 1) * BLOCK]
        ).astype(BF)
    total = jnp.sum(squares, axis=1, keepdims=True)
    high = total.astype(BF)
    low = (total - high.astype(F32)).astype(BF)
    lane = lax.broadcasted_iota(jnp.int32, (TOKENS, BLOCK), 1)
    both = jnp.where(
        lane < HALF,
        jnp.broadcast_to(high.astype(F32), (TOKENS, BLOCK)),
        jnp.broadcast_to(low.astype(F32), (TOKENS, BLOCK)),
    ).astype(BF)
    for out, k in zip(outs, SHIFTS):
        partial = lax.dot_general(
            scaled[...], kept_refs[k][...], NT, preferred_element_type=F32
        )
        out[:, :BLOCK] = (partial * SCALE).astype(BF)
        out[:, BLOCK : 2 * BLOCK] = both
    outs[-1][:, 2 * BLOCK :] = own_ref[...]


def layer(x, own, gain, kept):
    widths = [2 * BLOCK] * (Y - 1) + [3 * BLOCK]
    return pl.pallas_call(
        layer_kernel,
        out_shape=[jax.ShapeDtypeStruct((TOKENS, w), BF) for w in widths],
        scratch_shapes=[pltpu.VMEM((TOKENS, SPAN), BF)],
        compiler_params=SMALL,
        name="layer",
    )(x, own, gain, *kept)


def join(parts):
    projected = sum(p[:, :BLOCK].astype(F32) for p in parts)
    total = sum(
        p[:, BLOCK : BLOCK + 1].astype(F32) + p[:, BLOCK + HALF : BLOCK + HALF + 1].astype(F32)
        for p in parts
    )
    inverse = lax.rsqrt(total * (1.0 / D) + EPS)
    return (parts[-1][:, 2 * BLOCK :].astype(F32) + projected * inverse).astype(BF)


def mask_kernel(masks_ref, keep_ref):
    width = keep_ref.shape[1]
    keep_ref[...] = spread(masks_ref[...], pl.program_id(0) * width, width).astype(BF)


def spread_masks(masks):
    return pl.pallas_call(
        mask_kernel,
        grid=(Y,),
        in_specs=[pl.BlockSpec((ROWS, masks.shape[1]), lambda i: (0, 0))],
        out_specs=pl.BlockSpec((ROWS, SPAN), lambda i: (0, i)),
        out_shape=jax.ShapeDtypeStruct((ROWS, D), BF),
        compiler_params=SMALL,
        name="spread_masks",
    )(masks)


PER_STEP = 16
WIDTH = PER_STEP * BLOCK


def refit_kernel(
    x_ref, own_ref, gain_ref, weights_ref, keep_ref, inverse_ref, stream_ref, refit_ref,
    norm, acc, normed, met, turned,
):
    step = pl.program_id(0)

    @pl.when(step == 0)
    def _():
        def add(b, squares):
            x = x_ref[b].astype(F32)
            return squares + x * x

        squares = lax.fori_loop(0, D // BLOCK, add, jnp.zeros((TOKENS, BLOCK), F32), unroll=8)
        total = jnp.sum(squares, axis=1, keepdims=True)
        norm[...] = jnp.broadcast_to(lax.rsqrt(total * (1.0 / D) + EPS), (TOKENS, BLOCK))
        acc[...] = jnp.zeros((TOKENS, ROWS), F32)

    scale = norm[...]
    cuts = [slice(j * BLOCK, (j + 1) * BLOCK) for j in range(PER_STEP)]
    for j, cut in enumerate(cuts):
        x = x_ref[step * PER_STEP + j].astype(F32)
        normed[:, cut] = (x * scale * gain_ref[:, cut]).astype(BF)
    weights = weights_ref[...]
    keep = keep_ref[...]
    kept = weights * keep
    removed = weights - kept
    acc[...] += lax.dot_general(normed[...], kept, NT, preferred_element_type=F32)
    for j, cut in enumerate(cuts):
        product = lax.dot_general(
            removed[:, cut], normed[:, cut], NT, preferred_element_type=F32
        )
        met[:, cut] = (product * (1.0 / TOKENS)).astype(BF)
        turned[:, cut] = jnp.dot(
            normed[:, cut], inverse_ref[j], preferred_element_type=F32
        ).astype(BF)
    for cut in cuts:
        update = jnp.dot(met[:, cut], turned[:, cut], preferred_element_type=F32)
        refit_ref[:, cut] = (
            keep[:, cut].astype(F32) * (weights[:, cut].astype(F32) + update)
        ).astype(BF)

    @pl.when(step == D // WIDTH - 1)
    def _():
        stream_ref[...] = (own_ref[...].astype(F32) + acc[...] * SCALE).astype(BF)


def refit(x, own, gain, weights, keep, inverse):
    whole = lambda *shape: pl.BlockSpec(shape, lambda i: (0,) * len(shape))
    cut = lambda rows: pl.BlockSpec((rows, WIDTH), lambda i: (0, i))
    return pl.pallas_call(
        refit_kernel,
        grid=(D // WIDTH,),
        in_specs=[
            whole(D // BLOCK, TOKENS, BLOCK),
            whole(TOKENS, BLOCK),
            cut(1),
            cut(ROWS),
            cut(ROWS),
            pl.BlockSpec((PER_STEP, BLOCK, BLOCK), lambda i: (i, 0, 0)),
        ],
        out_specs=[whole(TOKENS, ROWS), cut(ROWS)],
        out_shape=[
            jax.ShapeDtypeStruct((TOKENS, ROWS), BF),
            jax.ShapeDtypeStruct((ROWS, D), BF),
        ],
        scratch_shapes=[pltpu.VMEM((TOKENS, BLOCK), F32), pltpu.VMEM((TOKENS, ROWS), F32)]
        + [pltpu.VMEM((ROWS, WIDTH), BF)] * 3,
        compiler_params=SMALL,
        name="refit",
    )(x, own, gain, weights, keep, inverse)


def to_next(section, shift, answer):
    moves = [(section, section + 1)]
    if answer and section in (2, 4, 6):
        moves.append((section - 1, section - 2))
    return [
        (source * Y * Z + y * Z + z, target * Y * Z + ((y + shift) % Y) * Z + z)
        for source, target in moves
        for y in range(Y)
        for z in range(Z)
    ]


def along_y(shift):
    return [
        (s * Y * Z + y * Z + z, s * Y * Z + ((y + shift) % Y) * Z + z)
        for s in range(SECTIONS)
        for y in range(Y)
        for z in range(Z)
    ]


def body(stream_in, gains, weights, masks, inv_hessian):
    section = lax.axis_index("section")
    y = lax.axis_index("dp") // Z
    rows = weights[0]
    mask_rows = masks[0]
    inverse_own = inv_hessian[0, 0].astype(BF)

    def gather_y(blocks):
        copies = jnp.broadcast_to(blocks[None], (Y,) + blocks.shape)
        got = lax.all_to_all(copies, "dp", 0, 0, axis_index_groups=Y_GROUPS)
        return got.reshape((Y * Z,) + blocks.shape[1:])

    def gather_z(own):
        copies = jnp.broadcast_to(own[None], (Z, TOKENS, BLOCK))
        return lax.all_to_all(copies, "dp", 0, 0, axis_index_groups=Z_GROUPS)

    kept = [keep_weights(lax.rem(y + k, Y), rows, mask_rows) for k in range(Y)]
    kept = [kept[0]] + [
        lax.ppermute(kept[Y - k], AXES, along_y(Y - k)) for k in range(1, Y)
    ]
    gain = lax.dynamic_slice_in_dim(gains, y * SPAN, SPAN, 1)

    own = stream_in
    mine = lax.cond(
        (section == 0) | (section >= 4),
        gather_z,
        lambda o: jnp.zeros((Z, TOKENS, BLOCK), BF),
        jnp.where(section == 0, own, inverse_own),
    )
    inverse_z = mine
    my_own = own
    inverse = jnp.zeros((Y * Z, BLOCK, BLOCK), BF)
    widths = [2 * BLOCK] * (Y - 1) + [3 * BLOCK]
    for phase in range(SECTIONS - 1):
        here = section == phase

        def active(mine, own, *kept):
            x = gather_z(own) if phase else mine
            return [x, *layer(x, own, gain, kept)]

        def idle(mine, own, *kept):
            return [mine] + [jnp.zeros((TOKENS, w), BF) for w in widths]

        mine, *messages = lax.cond(here, active, idle, mine, own, *kept)
        my_own = jnp.where(here, own, my_own)
        parts = [
            lax.ppermute(m, AXES, to_next(phase, k, k == 0)) for m, k in zip(messages, SHIFTS)
        ]
        if phase == 0:
            messages, inverse_z = lax.optimization_barrier((messages, inverse_z))
            inverse = lax.cond(section >= 4, lambda z, i: gather_y(z), lambda z, i: i, inverse_z, inverse)
            parts, inverse = lax.optimization_barrier((parts, inverse))
        if phase == 1:
            messages, mask_rows = lax.optimization_barrier((messages, mask_rows))
            keep = spread_masks(mask_rows)
            parts, keep = lax.optimization_barrier((parts, keep))
        if phase in (3, 5):
            messages, inverse_own = lax.optimization_barrier((messages, inverse_own))
            inverse = lax.cond(
                (section == phase - 3) | (section == phase - 2), lambda b, i: gather_y(gather_z(b)), lambda b, i: i, inverse_own, inverse
            )
            parts, inverse = lax.optimization_barrier((parts, inverse))
        own = join(parts)

    last = section == SECTIONS - 1
    mine = lax.cond(last, lambda m, o: gather_z(o), lambda m, o: m, mine, own)
    my_own = jnp.where(last, own, my_own)
    x = gather_y(mine)
    stream, refitted = refit(x, my_own, gains, rows, keep, inverse)
    return (stream[None], refitted[None])


def solution(mesh):
    placed = (
        P(None, "dp"),
        P("section", None),
        P("section", "dp", None),
        P("section", "dp", None),
        P("section", "dp", None, None),
    )
    return jax.shard_map(
        body,
        mesh=mesh,
        in_specs=placed,
        out_specs=(P("section", None, "dp"), P("section", "dp", None)),
        check_vma=False,
    )
```
